128 devices in a mesh: chan: 8 (over z, x_lo), tm: 16 (over y, x_hi, core).
Axes of the slice: x: 4 (x_hi: 2, x_lo: 2; x = x_hi * 2 + x_lo), y: 4, z: 4, core: 2. Of those that a mesh axis runs over, the one named last changes fastest.
Arguments:
- recording: bfloat16 [4096, 240000], P('chan', 'tm'), may hold values from -6 to 6
- offsets: int32 [32], replicated, may hold values from 0 to 3749, as said below
- band_bins: int32 [20], replicated, may hold values from 61 to 300
- dead_flags: int32 [4096], P('chan'), may hold values 0 or 1
Outputs:
- stacks: bfloat16 [2, 20, 4096, 4096], P(None, None, 'tm', 'chan')
The draws below stay inside these ranges and needn't reach their ends.
Inputs may be any that keep to these rules, and one draw needn't show every extreme that they name: `offsets`: every window's offset is drawn afresh; the last window of some block of 2 consecutive windows has the largest offset.
All inputs are finite; a program needn't handle non-finite values. No bound on the sum of `dead_flags` on one device may be relied on, other than what follows from the above.
Results may differ from the reference program's by a relative error of at most 0.0063.
Values may be sent and summed in bfloat16 or wider, within the bound.
A program may use at most 128 MiB of HBM per device.

```python
import math
import jax
import jax.numpy as jnp
from jax import lax

CH = 4096
L = 15000
NB = 20
W_DEV = 2
WIN = 32
SAMPLES = 240000


def draw_offsets(key, part):
    off_limit = L // 4
    key_values, key_place = jax.random.split(key)
    values = jax.random.randint(key_values, (WIN,), 0, off_limit, dtype=jnp.int32)
    device = jax.random.randint(key_place, (), 0, WIN // W_DEV, dtype=jnp.int32)
    return values.at[device * W_DEV + W_DEV - 1].set(off_limit - 1)


def touch_ends(array, rng, least, high):
    place = [jax.random.randint(jax.random.fold_in(rng, axis), (), 0, length) for axis, length in enumerate(array.shape)]
    widest = array.shape.index(max(array.shape))
    beside = place[:widest] + [(place[widest] + 1) % array.shape[widest]] + place[widest + 1:]
    return array.at[tuple(place)].set(least).at[tuple(beside)].set(high)


def block_levels(stream_key, shape, pieces, low, largest):
    def one(position, blocks):
        steps = jax.random.uniform(jax.random.fold_in(jax.random.fold_in(stream_key, 6), position), (blocks,), jnp.float32, low / len(pieces), largest / len(pieces))
        return jnp.repeat(jnp.exp(steps), shape[position] // blocks).reshape((-1,) + (1,) * (len(shape) - position - 1))

    factor_of = one(*pieces[0])
    for cut in pieces[1:]:
        factor_of = factor_of * one(*cut)
    return factor_of


def scatter_about(stream_key, shape, scale, limit, pieces=(), kind=jnp.bfloat16):
    loudness = block_levels(stream_key, shape, pieces, -0.22, 0.18) if pieces else 1.0
    drawn = jax.random.normal(stream_key, shape, jnp.float32) * scale * loudness
    return jnp.minimum(jnp.maximum(drawn, -limit), limit).astype(kind)


def setup_inputs(seed: int = 0) -> dict:
    keys = jax.random.split(jax.random.key(seed), 5)
    recording = scatter_about(keys[0], (CH, SAMPLES), 1.0, 6.0, ((0, 8), (1, 16)))
    offsets = draw_offsets(jax.random.fold_in(keys[4], 71), 0)
    band_bins = touch_ends(jax.random.randint(keys[2], (NB,), L // 250 + 1, L // 50 + 1), jax.random.fold_in(keys[2], 1), L // 250 + 1, (L // 50 + 1) - 1).astype(jnp.int32)
    dead_flags = touch_ends((jax.random.randint(keys[3], (CH,), 0, 16) < 1).astype(jnp.int32), jax.random.fold_in(keys[3], 1), 0, 1)
    return dict(recording=recording, offsets=offsets, band_bins=band_bins, dead_flags=dead_flags)


TWO_PI = 2.0 * math.pi
FLOOR = 0.7

def dft_rows(band_bins):
    sample_index = jnp.arange(L, dtype=jnp.int32)
    turn_index = band_bins[:, None] * sample_index[None, :] % L
    angles = turn_index.astype(jnp.float32) * (TWO_PI / L)
    norm_scale = 1.0 / math.sqrt(L)
    return jnp.concatenate([jnp.cos(angles) * norm_scale, -jnp.sin(angles) * norm_scale], axis=0).astype(jnp.bfloat16)

def reference(recording, offsets, band_bins, dead_flags):
    hop_size = L // 2
    rim_width = hop_size + hop_size // 2
    dft_table = dft_rows(band_bins).astype(jnp.float32)
    alive = (1 - dead_flags).astype(jnp.float32)
    last_start = SAMPLES - L
    tail_region = jnp.concatenate([recording[:, last_start:], jnp.zeros((CH, rim_width), jnp.bfloat16)], axis=1)

    def one_window(index):
        start = (index * hop_size + offsets[index]).astype(jnp.int32)
        main_piece = lax.dynamic_slice_in_dim(recording, jnp.minimum(start, last_start).astype(jnp.int32), L, 1)
        tail_piece = lax.dynamic_slice_in_dim(tail_region, jnp.maximum(start - last_start, 0).astype(jnp.int32), L, 1)
        piece = jnp.where(start > last_start, tail_piece, main_piece).astype(jnp.float32)
        raw_spectra = lax.dot_general(dft_table, piece, (((1,), (1,)), ((), ())), precision=lax.Precision.HIGHEST)
        energy = lax.optimization_barrier(jnp.sum(piece * piece, axis=1))
        spectra = raw_spectra / jnp.sqrt(energy / L + 1e-06)[None, :]
        level = lax.optimization_barrier(jnp.mean(spectra * spectra, axis=0)) * 2.0
        factor = alive / jnp.sqrt(jnp.maximum(level, FLOOR))
        return (spectra * factor[None, :]).astype(jnp.bfloat16).reshape(2, NB, CH)
    white = lax.map(one_window, jnp.arange(WIN, dtype=jnp.int32))
    stack_scale = 1.0 / math.sqrt(WIN)

    def one_bin(index):
        part_now = lax.dynamic_index_in_dim(white, index, 2, keepdims=False).astype(jnp.float32)
        real_part = jnp.einsum('wpj,wpi->ji', part_now, part_now, precision=lax.Precision.HIGHEST)
        flipped = jnp.stack([-part_now[:, 1], part_now[:, 0]], axis=1)
        imag_part = jnp.einsum('wpj,wpi->ji', flipped, part_now, precision=lax.Precision.HIGHEST)
        return (jnp.stack([real_part, imag_part]) * stack_scale).astype(jnp.bfloat16)
    per_bin = lax.map(one_bin, jnp.arange(NB, dtype=jnp.int32))
    return jnp.swapaxes(per_bin, 0, 1)
```

```python
import functools
import math

import jax
import jax.numpy as jnp
from jax import lax
from jax.experimental import pallas as pl
from jax.experimental.pallas import tpu as pltpu
from jax.sharding import PartitionSpec as P

L = 15000
NB = 20
HOP = L // 2
TWO_PI = 2.0 * math.pi
FLOOR = 0.7
WIN = 32
STEP = 1024
CHUNKS = 15
ROWS = 40
F32 = jnp.float32
BF16 = jnp.bfloat16


def bin_rows(bins):
    row = lax.broadcasted_iota(jnp.int32, (24, 128), 0)
    out = jnp.zeros((24, 128), jnp.int32)
    for b in range(NB):
        hit = row == b
        if b >= 16:
            hit = hit | (row == b + 4)
        out = jnp.where(hit, bins[b], out)
    return out.astype(F32)


def turned(turns):
    whole = jnp.floor(turns * (1.0 / L))
    rest = turns - whole * float(L)
    rest = jnp.where(rest < 0.0, rest + float(L), rest)
    rest = jnp.where(rest >= float(L), rest - float(L), rest)
    angle = rest * (TWO_PI / L)
    return jnp.cos(angle), jnp.sin(angle)


def start_state(bins, first):
    lane = lax.broadcasted_iota(jnp.int32, (24, 128), 1)
    row = lax.broadcasted_iota(jnp.int32, (24, 128), 0)
    place = (lane + (first + L)).astype(F32)
    quarter = jnp.where(row >= 20, float(L // 4), 0.0)
    cosine, sine = turned(bins * place + quarter)
    scale = 1.0 / math.sqrt(L)
    return cosine * scale, -sine * scale


def turn_on(state, step):
    v, q = state
    c, s = step
    return v * c + q * s, q * c - v * s


def table_rows(state, keep):
    v, q = state
    rows = jnp.concatenate([v[:16], q[:16], v[16:]], axis=0)
    return rows if keep is None else jnp.where(keep, rows, 0.0)


def local_sums(x_hbm, offs, bins_ref, part, xbuf, tab, sems):
    t = lax.axis_index("tm")

    def chunk_copy(g):
        rows = STEP if isinstance(g, jax.Array) or g < CHUNKS - 1 else L - STEP * (CHUNKS - 1)
        at = pl.ds(pl.multiple_of(g * STEP, STEP), rows)
        return pltpu.make_async_copy(x_hbm.at[at], xbuf.at[at], sems.at[g])

    tail = (L // 16) * 16
    xbuf[pl.ds(tail, CHUNKS * STEP - tail)] = jnp.zeros((CHUNKS * STEP - tail, 512), BF16)
    for g in range(CHUNKS):
        chunk_copy(g).start()

    before = 2 * jnp.maximum(t - 1, 0)
    off0, off1 = offs[2 * t], offs[2 * t + 1]
    boff0, boff1 = offs[before], offs[before + 1]
    a0, a1 = off0, HOP + off1
    e0, e1 = boff0, HOP + boff1

    bins = bin_rows(bins_ref)
    step = turned(bins * 128.0)
    part[...] = jnp.zeros_like(part)

    low = jnp.zeros((16, STEP), jnp.int32)
    high = jnp.zeros((16, STEP), jnp.int32)
    row = lax.broadcasted_iota(jnp.int32, (16, STEP), 0)
    for r, (lo, hi) in enumerate(((a0, L), (a1, L), (0, e0), (0, e1))):
        low = jnp.where(row == r, lo, low)
        high = jnp.where(row == r, hi, high)
    inner = lax.broadcasted_iota(jnp.int32, (16, STEP), 1)
    lane = lax.broadcasted_iota(jnp.int32, (ROWS, 128), 1)

    def chunk(g, states, slots):
        states = list(states)
        for k in range(STEP // 128):
            place = lane + (g * STEP + k * 128)
            rows = []
            for n, (_, limit) in enumerate(slots):
                keep = None
                if limit is not None:
                    keep = place >= limit[1] if limit[0] else place < limit[1]
                rows.append(table_rows(states[n], keep))
                states[n] = turn_on(states[n], step)
            if len(slots) == 3:
                rows.append(jnp.zeros((8, 128), F32))
            made = jnp.concatenate(rows, axis=0).astype(BF16)
            tab[0 : made.shape[0], k * 128 : (k + 1) * 128] = made
        chunk_copy(g).wait()
        height = 128 if len(slots) == 3 else 80
        x = xbuf[pl.ds(pl.multiple_of(g * STEP, STEP), STEP), :]
        raw = jnp.dot(tab[0:height, :], x, preferred_element_type=F32)
        place = inner + g * STEP
        mask = jnp.where((place >= low) & (place < high), 1.0, 0.0).astype(BF16)
        square = jnp.dot(mask, x * x, preferred_element_type=F32)
        for n, (target, _) in enumerate(slots):
            half, w = target
            part[half, w * ROWS : (w + 1) * ROWS] += raw[n * ROWS : (n + 1) * ROWS]
        part[0, 80:88] += square[0:8]
        return tuple(states)

    own0, own1, back0, back1 = (0, 0), (0, 1), (1, 0), (1, 1)
    s_own0 = start_state(bins, -a0)
    s_back0 = start_state(bins, L - e0)
    s_back1 = start_state(bins, L - e1)
    s_own1 = start_state(bins, 7 * STEP - a1)

    slots = ((own0, (True, a0)), (back1, None), (back0, (False, e0)))
    s_own0, s_back1, _ = lax.fori_loop(
        0, 4, lambda g, s: chunk(g, s, slots), (s_own0, s_back1, s_back0)
    )
    slots1 = ((own0, None), (back1, None))
    s_own0, s_back1 = lax.fori_loop(4, 7, lambda g, s: chunk(g, s, slots1), (s_own0, s_back1))
    slots2 = ((own0, None), (back1, (False, e1)), (own1, (True, a1)))
    s_own0, _, s_own1 = lax.fori_loop(
        7, 11, lambda g, s: chunk(g, s, slots2), (s_own0, s_back1, s_own1)
    )
    slots3 = ((own0, None), (own1, None))
    states = lax.fori_loop(11, 14, lambda g, s: chunk(g, s, slots3), (s_own0, s_own1))
    chunk(14, states, slots3)
    part[1, 80:82] = part[0, 82:84]


def local_call(x, offsets, band_bins):
    return pl.pallas_call(
        local_sums,
        out_shape=jax.ShapeDtypeStruct((2, 88, 512), F32),
        in_specs=[
            pl.BlockSpec(memory_space=pl.ANY),
            pl.BlockSpec(memory_space=pltpu.SMEM),
            pl.BlockSpec(memory_space=pltpu.SMEM),
        ],
        out_specs=pl.BlockSpec(memory_space=pltpu.VMEM),
        scratch_shapes=[
            pltpu.VMEM((CHUNKS * STEP, 512), BF16),
            pltpu.VMEM((128, STEP), BF16),
            pltpu.SemaphoreType.DMA((CHUNKS,)),
        ],
        compiler_params=pltpu.CompilerParams(vmem_limit_bytes=48 << 20),
        name="local_sums",
    )(x, offsets, band_bins)


def whitened(total, dead):
    alive = 1.0 - dead.astype(F32)
    out = []
    for w in range(2):
        raw = total[w * ROWS : (w + 1) * ROWS]
        energy = total[80 + w : 81 + w]
        spectra = raw / jnp.sqrt(energy / L + 1e-06)
        level = jnp.sum(spectra * spectra, axis=0, keepdims=True) * (1.0 / NB)
        out.append(spectra * (alive / jnp.sqrt(jnp.maximum(level, FLOOR))))
    return jnp.concatenate(out, axis=0).astype(BF16)


def regroup():
    d = lax.broadcasted_iota(jnp.int32, (80, 80), 0)
    s = lax.broadcasted_iota(jnp.int32, (80, 80), 1)
    p, w = (d >> 3) & 1, (d >> 2) & 1
    b = (d >> 4) * 4 + (d & 3)
    source = w * ROWS + jnp.where(b < 16, p * 16 + b, 32 + p * 4 + (b - 16))
    return jnp.where(s == source, 1.0, 0.0).astype(BF16)


def exchange(part, dead, gi, gj, back, send_sems, back_sems, i_sems, j_sems):
    c = lax.axis_index("chan")
    t = lax.axis_index("tm")
    z, xl = c // 2, c % 2
    y, xh, core = t // 4, (t // 2) % 2, t % 2
    sent = []

    def send(source, target, recv, device):
        copy = pltpu.make_async_remote_copy(
            src_ref=source,
            dst_ref=target,
            send_sem=send_sems.at[len(sent)],
            recv_sem=recv,
            device_id=device,
            device_id_type=pl.DeviceIdType.MESH,
        )
        copy.start()
        sent.append(copy)

    def block_of(yy, hi, k):
        return 4 * (yy % 4) + 2 * hi + k

    up, down = (c, block_of(y + 1, xh, core)), (c, block_of(y + 3, xh, core))
    across, other = (c, block_of(y, 1 - xh, core)), (c, block_of(y, xh, 1 - core))
    z_up, z_down = ((c + 2) % 8, t), ((c + 6) % 8, t)
    previous, following = (c, (t + 15) % 16), (c, (t + 1) % 16)

    barrier = pltpu.get_barrier_semaphore()
    sources = [up, down, across, other, z_up, z_down, following]
    sources += [(2 * y + xh, block_of(z + 2, hi, k)) for hi in range(2) for k in range(2)]
    for device in sources:
        pl.semaphore_signal(
            barrier, inc=1, device_id=device, device_id_type=pl.DeviceIdType.MESH
        )
    pl.semaphore_wait(barrier, len(sources))

    send(part.at[1], back, back_sems.at[0], previous)
    matrix = regroup()
    sent[0].wait_recv()
    more = jnp.where(t == 15, 0.0, back[...])
    white = whitened(part[0] + more, dead[...])
    ordered = jnp.dot(matrix, white, preferred_element_type=F32).astype(BF16)
    for h in range(2):
        gi[t, h] = ordered[:, h * 256 : (h + 1) * 256]

    def give(block, h, device):
        send(gi.at[block, h], gi.at[block, h], i_sems.at[block, h], device)

    def got(block, h):
        pltpu.make_async_copy(gi.at[block, h], gi.at[block, h], i_sems.at[block, h]).wait()

    def pass_j(q, s, device):
        send(gj.at[q, s], gj.at[q, s], j_sems.at[q, s], device)

    def got_j(q, s):
        pltpu.make_async_copy(gj.at[q, s], gj.at[q, s], j_sems.at[q, s]).wait()

    halves = range(2)
    for h in halves:
        give(t, h, across)
    for lo in halves:
        for h in halves:
            send(
                gi.at[t, h],
                gj.at[t // 2, core],
                j_sems.at[t // 2, core],
                (2 * ((y + 2) % 4) + lo, block_of(z, xl, h)),
            )
    for h in halves:
        give(t, h, up)
        give(t, h, down)
    for h in halves:
        give(t, h, other)

    near = block_of(y, 1 - xh, core)
    below, above = block_of(y + 3, xh, core), block_of(y + 1, xh, core)
    far = block_of(y + 2, xh, core)
    near_below, near_above = block_of(y + 3, 1 - xh, core), block_of(y + 1, 1 - xh, core)
    near_far = block_of(y + 2, 1 - xh, core)

    got(below, 0)
    give(below, 0, up)
    got(above, 1)
    give(above, 1, down)
    for h in halves:
        got(near, h)
        give(near, h, up)
        give(near, h, down)
    q_own = [2 * ((z + 2) % 4) + hi for hi in range(2)]
    q_low = [2 * ((z + 1) % 4) + hi for hi in range(2)]
    q_high = [2 * ((z + 3) % 4) + hi for hi in range(2)]
    q_far = [2 * z + hi for hi in range(2)]
    for q in q_own:
        for s in halves:
            got_j(q, s)
            pass_j(q, s, z_up)
            pass_j(q, s, z_down)
    got(below, 1)
    got(above, 0)
    for block in (below, above, near):
        for h in halves:
            give(block, h, other)
    got(near_below, 0)
    give(near_below, 0, up)
    got(near_above, 1)
    give(near_above, 1, down)
    for q_l, q_h in zip(q_low, q_high):
        got_j(q_l, 0)
        pass_j(q_l, 0, z_up)
        got_j(q_h, 1)
        pass_j(q_h, 1, z_down)
    got(near_below, 1)
    got(near_above, 0)
    for block in (near_below, near_above):
        for h in halves:
            give(block, h, other)
    for block in (far, near_far):
        for h in halves:
            got(block, h)
            give(block, h, other)
    for q_l, q_h in zip(q_low, q_high):
        got_j(q_l, 1)
        got_j(q_h, 0)
    for q in q_far:
        for s in halves:
            got_j(q, s)
    for yy in range(4):
        for hi in range(2):
            for h in halves:
                got(block_of(yy, hi, 1 - core), h)
    for copy in sent:
        copy.wait_send()


N_SENDS = 1 + 2 + 4 + 4 + 2 + 2 + 4 + 8 + 6 + 2 + 4 + 4 + 4


def exchange_call(part, dead):
    vmem = pl.BlockSpec(memory_space=pltpu.VMEM)
    return pl.pallas_call(
        exchange,
        out_shape=(
            jax.ShapeDtypeStruct((16, 2, 80, 256), BF16),
            jax.ShapeDtypeStruct((8, 2, 80, 256), BF16),
        ),
        in_specs=[vmem, vmem],
        out_specs=(vmem, vmem),
        scratch_shapes=[
            pltpu.VMEM((88, 512), F32),
            pltpu.SemaphoreType.DMA((N_SENDS,)),
            pltpu.SemaphoreType.DMA((1,)),
            pltpu.SemaphoreType.DMA((16, 2)),
            pltpu.SemaphoreType.DMA((8, 2)),
        ],
        compiler_params=pltpu.CompilerParams(collective_id=0, has_side_effects=True),
        name="exchange",
    )(part, dead)


def stack_group(gi, gj, out, lhs):
    xj = gj[...].reshape(16, 16, 256).astype(F32)
    flipped = jnp.concatenate([-xj[:, 8:], xj[:, :8]], axis=1)
    bin_of = lax.broadcasted_iota(jnp.int32, (256, 256), 1) & 3
    for s, rows in enumerate((xj, flipped)):
        turned_rows = rows.reshape(256, 256).T
        for b in range(4):
            at = (s * 4 + b) * 256
            lhs[at : at + 256] = jnp.where(bin_of == b, turned_rows, 0.0).astype(BF16)
    scale = 1.0 / math.sqrt(WIN)
    for h in range(2):
        right = gi[:, h].reshape(256, 256)
        for s in range(2):
            for b in range(4):
                at = (s * 4 + b) * 256
                made = jnp.dot(lhs[at : at + 256], right, preferred_element_type=F32)
                out[s, b, :, h * 256 : (h + 1) * 256] = (made * scale).astype(BF16)


def stack_call(gi, gj):
    return pl.pallas_call(
        stack_group,
        out_shape=jax.ShapeDtypeStruct((2, NB, 256, 512), BF16),
        grid=(5,),
        in_specs=[
            pl.BlockSpec((16, 2, 16, 256), lambda g: (0, 0, g, 0)),
            pl.BlockSpec((8, 2, 16, 256), lambda g: (0, 0, g, 0)),
        ],
        out_specs=pl.BlockSpec((2, 4, 256, 512), lambda g: (0, g, 0, 0)),
        scratch_shapes=[pltpu.VMEM((2048, 256), BF16)],
        name="stack",
    )(gi, gj)


def shards(recording, offsets, band_bins, dead_flags):
    part = local_call(recording.T, offsets, band_bins)
    gi, gj = exchange_call(part, dead_flags.reshape(1, -1))
    return stack_call(gi, gj)


def solution(mesh):
    return jax.shard_map(
        shards,
        mesh=mesh,
        in_specs=(P("chan", "tm"), P(), P(), P("chan")),
        out_specs=P(None, None, "tm", "chan"),
        check_vma=False,
    )
```

```python
import functools
import math

import jax
import jax.numpy as jnp
from jax import lax
from jax.experimental import pallas as pl
from jax.experimental.pallas import tpu as pltpu
from jax.sharding import PartitionSpec as P

L = 15000
NB = 20
HOP = L // 2
TWO_PI = 2.0 * math.pi
FLOOR = 0.7
WIN = 32
STEP = 1024
CHUNKS = 15
ROWS = 40
AHEAD = 6
F32 = jnp.float32
BF16 = jnp.bfloat16


def bin_rows(bins):
    row = lax.broadcasted_iota(jnp.int32, (24, 128), 0)
    out = jnp.zeros((24, 128), jnp.int32)
    for b in range(NB):
        hit = row == b
        if b >= 16:
            hit = hit | (row == b + 4)
        out = jnp.where(hit, bins[b], out)
    return out.astype(F32)


def turned(turns):
    whole = jnp.floor(turns * (1.0 / L))
    rest = turns - whole * float(L)
    rest = jnp.where(rest < 0.0, rest + float(L), rest)
    rest = jnp.where(rest >= float(L), rest - float(L), rest)
    angle = rest * (TWO_PI / L)
    return jnp.cos(angle), jnp.sin(angle)


def start_state(bins, first):
    lane = lax.broadcasted_iota(jnp.int32, (24, 128), 1)
    row = lax.broadcasted_iota(jnp.int32, (24, 128), 0)
    place = (lane + (first + L)).astype(F32)
    quarter = jnp.where(row >= 20, float(L // 4), 0.0)
    cosine, sine = turned(bins * place + quarter)
    scale = 1.0 / math.sqrt(L)
    return cosine * scale, -sine * scale


def turn_on(state, step):
    v, q = state
    c, s = step
    return v * c + q * s, q * c - v * s


def table_rows(state, keep):
    v, q = state
    rows = jnp.concatenate([v[:16], q[:16], v[16:]], axis=0)
    return rows if keep is None else jnp.where(keep, rows, 0.0)


def regroup():
    d = lax.broadcasted_iota(jnp.int32, (80, 80), 0)
    s = lax.broadcasted_iota(jnp.int32, (80, 80), 1)
    p, w = (d >> 3) & 1, (d >> 2) & 1
    b = (d >> 4) * 4 + (d & 3)
    source = w * ROWS + jnp.where(b < 16, p * 16 + b, 32 + p * 4 + (b - 16))
    return jnp.where(s == source, 1.0, 0.0).astype(BF16)


def front(
    x_hbm, offs_hbm, bins_hbm, dead_hbm, gi, gj,
    xbuf, tab, offs, bins_ref, dead, own, sums, back, recv,
    x_sems, small_sems, send_sems, back_sems, i_sems, j_sems,
):
    c = lax.axis_index("chan")
    t = lax.axis_index("tm")
    z, xl = c // 2, c % 2
    y, xh, core = t // 4, (t // 2) % 2, t % 2
    sent = []

    def send(source, target, recv_sem, device):
        copy = pltpu.make_async_remote_copy(
            src_ref=source,
            dst_ref=target,
            send_sem=send_sems.at[len(sent)],
            recv_sem=recv_sem,
            device_id=device,
            device_id_type=pl.DeviceIdType.MESH,
        )
        copy.start()
        sent.append(copy)
        return copy

    def block_of(yy, hi, k):
        return 4 * (yy % 4) + 2 * hi + k

    up, down = (c, block_of(y + 1, xh, core)), (c, block_of(y + 3, xh, core))
    across, other = (c, block_of(y, 1 - xh, core)), (c, block_of(y, xh, 1 - core))
    z_up, z_down = ((c + 2) % 8, t), ((c + 6) % 8, t)
    previous, following = (c, (t + 15) % 16), (c, (t + 1) % 16)

    barrier = pltpu.get_barrier_semaphore()
    sources = [up, down, across, other, z_up, z_down, following]
    sources += [(2 * y + xh, block_of(2 * y + 6 - z, hi, k)) for hi in range(2) for k in range(2)]
    for device in sources:
        pl.semaphore_signal(
            barrier, inc=1, device_id=device, device_id_type=pl.DeviceIdType.MESH
        )

    small = [
        pltpu.make_async_copy(src, dst, small_sems.at[n])
        for n, (src, dst) in enumerate(((offs_hbm, offs), (bins_hbm, bins_ref), (dead_hbm, dead)))
    ]
    for copy in small:
        copy.start()

    def chunk_copy(g):
        rows = STEP if isinstance(g, jax.Array) or g < CHUNKS - 1 else L - STEP * (CHUNKS - 1)
        at = pl.ds(pl.multiple_of(g * STEP, STEP), rows)
        return pltpu.make_async_copy(x_hbm.at[at], xbuf.at[at], x_sems.at[g])

    tail = (L // 16) * 16
    for g in range(AHEAD):
        chunk_copy(g).start()
    xbuf[pl.ds(tail, CHUNKS * STEP - tail)] = jnp.zeros((CHUNKS * STEP - tail, 512), BF16)
    own[...] = jnp.zeros_like(own)
    back[...] = jnp.zeros_like(back)
    sums[...] = jnp.zeros_like(sums)
    for copy in small:
        copy.wait()

    before = 2 * jnp.maximum(t - 1, 0)
    off0, off1 = offs[2 * t], offs[2 * t + 1]
    boff0, boff1 = offs[before], offs[before + 1]
    a0, a1 = off0, HOP + off1
    e0, e1 = boff0, HOP + boff1
    bins = bin_rows(bins_ref)
    step = turned(bins * 128.0)

    low = jnp.zeros((16, STEP), jnp.int32)
    high = jnp.zeros((16, STEP), jnp.int32)
    row = lax.broadcasted_iota(jnp.int32, (16, STEP), 0)
    for r, (lo, hi) in enumerate(((a0, L), (a1, L), (0, e0), (0, e1))):
        low = jnp.where(row == r, lo, low)
        high = jnp.where(row == r, hi, high)
    inner = lax.broadcasted_iota(jnp.int32, (16, STEP), 1)
    lane = lax.broadcasted_iota(jnp.int32, (ROWS, 128), 1)

    def chunk(g, slot, states, limits, targets, energies):
        states = list(states)
        tables = len(limits)
        height = 48 if tables == 1 else 80
        for k in range(STEP // 128):
            place = lane + (g * STEP + k * 128)
            rows = []
            for n, limit in enumerate(limits):
                keep = None
                if limit is not None:
                    keep = place >= limit[1] if limit[0] else place < limit[1]
                rows.append(table_rows(states[n], keep))
                states[n] = turn_on(states[n], step)
            if tables == 1:
                rows.append(jnp.zeros((8, 128), F32))
            tab[slot, 0:height, k * 128 : (k + 1) * 128] = jnp.concatenate(rows, axis=0).astype(BF16)
        x = xbuf[pl.ds(pl.multiple_of(g * STEP, STEP), STEP), :]
        raw = jnp.dot(tab[slot, 0:height, :], x, preferred_element_type=F32)
        for n, target in enumerate(targets):
            target[0:ROWS] += raw[n * ROWS : (n + 1) * ROWS]
        if energies:
            place = inner + g * STEP
            mask = jnp.where((place >= low) & (place < high), 1.0, 0.0).astype(BF16)
            sums[...] += jnp.dot(mask, x * x, preferred_element_type=F32)[0:8]
        return tuple(states)

    own0, own1 = own.at[0], own.at[1]
    back0, back1 = back.at[0], back.at[1]
    states = (start_state(bins, L - e0), start_state(bins, L - e1))
    for g in range(4):
        chunk_copy(g).wait()
        if g + AHEAD < CHUNKS:
            chunk_copy(g + AHEAD).start()
        states = chunk(g, g % 2, states, ((False, e0), None), (back0, back1), True)
    back[0, 40:41] = sums[2:3]
    pl.semaphore_wait(barrier, len(sources))
    early = send(back.at[0], recv.at[0], back_sems.at[0], previous)
    states = states[1:]
    s_own0 = start_state(bins, -a0)
    s_own1 = start_state(bins, 7 * STEP - a1)
    chunk_copy(4).wait()
    for g in range(4 + AHEAD, CHUNKS):
        chunk_copy(g).start()
    states = chunk(4, 0, states, ((False, e1),), (back1,), True)

    def pair(i, states):
        for k in range(2):
            chunk_copy(5 + 2 * i + k).wait()
        for k in range(2):
            states = chunk(5 + 2 * i + k, 1 - k, states, ((False, e1),), (back1,), True)
        return states

    lax.fori_loop(0, 3, pair, states)
    back[1, 40:41] = sums[3:4]
    late = send(back.at[1], recv.at[1], back_sems.at[1], previous)

    states = chunk(0, 0, (s_own0,), ((True, a0),), (own0,), False)

    def pair_own(i, states):
        for k in range(2):
            states = chunk(1 + 2 * i + k, 1 - k, states, ((True, a0),), (own0,), False)
        return states

    states = lax.fori_loop(0, 3, pair_own, states)
    for g in range(11, CHUNKS):
        chunk_copy(g).wait()
    both = (None, (True, a1))
    def pair_both(i, states):
        for k in range(2):
            states = chunk(7 + 2 * i + k, k, states, both, (own0, own1), False)
        return states

    def pair_last(i, states):
        for k in range(2):
            states = chunk(11 + 2 * i + k, k, states, both, (own0, own1), True)
        return states

    states = lax.fori_loop(0, 2, pair_both, states + (s_own1,))
    lax.fori_loop(0, 2, pair_last, states)

    matrix = regroup()
    alive = 1.0 - dead[...].astype(F32)
    early.wait_recv()
    late.wait_recv()
    white = []
    for w in range(2):
        more = jnp.where(t == 15, 0.0, recv[w])
        raw = own[w, 0:ROWS] + more[0:ROWS]
        energy = sums[w : w + 1] + more[40:41]
        spectra = raw / jnp.sqrt(energy / L + 1e-06)
        level = jnp.sum(spectra * spectra, axis=0, keepdims=True) * (1.0 / NB)
        white.append(spectra * (alive / jnp.sqrt(jnp.maximum(level, FLOOR))))
    white = jnp.concatenate(white, axis=0).astype(BF16)
    ordered = jnp.dot(matrix, white, preferred_element_type=F32).astype(BF16)
    for h in range(2):
        gi[t, h] = ordered[:, h * 256 : (h + 1) * 256]

    def give(block, h, device):
        send(gi.at[block, h], gi.at[block, h], i_sems.at[block, h], device)

    def got(block, h):
        pltpu.make_async_copy(gi.at[block, h], gi.at[block, h], i_sems.at[block, h]).wait()

    def pass_j(q, s, device):
        send(gj.at[q, s], gj.at[q, s], j_sems.at[q, s], device)

    def got_j(q, s):
        pltpu.make_async_copy(gj.at[q, s], gj.at[q, s], j_sems.at[q, s]).wait()

    halves = range(2)
    for h in halves:
        give(t, h, across)
    for lo in halves:
        for h in halves:
            send(
                gi.at[t, h],
                gj.at[t // 2, core],
                j_sems.at[t // 2, core],
                (2 * ((2 * z + 6 - y) % 4) + lo, block_of(z, xl, h)),
            )
    for h in halves:
        give(t, h, up)
        give(t, h, down)
    for h in halves:
        give(t, h, other)

    near = block_of(y, 1 - xh, core)
    below, above = block_of(y + 3, xh, core), block_of(y + 1, xh, core)
    far = block_of(y + 2, xh, core)
    near_below, near_above = block_of(y + 3, 1 - xh, core), block_of(y + 1, 1 - xh, core)
    near_far = block_of(y + 2, 1 - xh, core)

    got(below, 0)
    give(below, 0, up)
    got(above, 1)
    give(above, 1, down)
    for h in halves:
        got(near, h)
        give(near, h, up)
        give(near, h, down)
    q_own = [2 * ((2 * y + 6 - z) % 4) + hi for hi in range(2)]
    q_low = [2 * ((2 * y + 7 - z) % 4) + hi for hi in range(2)]
    q_high = [2 * ((2 * y + 5 - z) % 4) + hi for hi in range(2)]
    q_far = [2 * ((2 * y + 8 - z) % 4) + hi for hi in range(2)]
    for q in q_own:
        for s in halves:
            got_j(q, s)
            pass_j(q, s, z_up)
            pass_j(q, s, z_down)
    got(below, 1)
    got(above, 0)
    for block in (below, above, near):
        for h in halves:
            give(block, h, other)
    got(near_below, 0)
    give(near_below, 0, up)
    got(near_above, 1)
    give(near_above, 1, down)
    for q_l, q_h in zip(q_low, q_high):
        got_j(q_l, 0)
        pass_j(q_l, 0, z_up)
        got_j(q_h, 1)
        pass_j(q_h, 1, z_down)
    got(near_below, 1)
    got(near_above, 0)
    for block in (near_below, near_above):
        for h in halves:
            give(block, h, other)
    for block in (far, near_far):
        for h in halves:
            got(block, h)
            give(block, h, other)
    for q_l, q_h in zip(q_low, q_high):
        got_j(q_l, 1)
        got_j(q_h, 0)
    for q in q_far:
        for s in halves:
            got_j(q, s)
    for yy in range(4):
        for hi in range(2):
            for h in halves:
                got(block_of(yy, hi, 1 - core), h)
    for copy in sent:
        copy.wait_send()


N_SENDS = 48


def front_call(x, offsets, band_bins, dead):
    anywhere = pl.BlockSpec(memory_space=pltpu.HBM)
    vmem = pl.BlockSpec(memory_space=pltpu.VMEM)
    return pl.pallas_call(
        front,
        out_shape=(
            jax.ShapeDtypeStruct((16, 2, 80, 256), BF16),
            jax.ShapeDtypeStruct((8, 2, 80, 256), BF16),
        ),
        in_specs=[anywhere] * 4,
        out_specs=(vmem, vmem),
        scratch_shapes=[
            pltpu.VMEM((CHUNKS * STEP, 512), BF16),
            pltpu.VMEM((2, 80, STEP), BF16),
            pltpu.SMEM((32,), jnp.int32),
            pltpu.SMEM((NB,), jnp.int32),
            pltpu.VMEM((1, 512), jnp.int32),
            pltpu.VMEM((2, ROWS, 512), F32),
            pltpu.VMEM((8, 512), F32),
            pltpu.VMEM((2, 48, 512), F32),
            pltpu.VMEM((2, 48, 512), F32),
            pltpu.SemaphoreType.DMA((CHUNKS,)),
            pltpu.SemaphoreType.DMA((3,)),
            pltpu.SemaphoreType.DMA((N_SENDS,)),
            pltpu.SemaphoreType.DMA((2,)),
            pltpu.SemaphoreType.DMA((16, 2)),
            pltpu.SemaphoreType.DMA((8, 2)),
        ],
        compiler_params=pltpu.CompilerParams(
            collective_id=0, has_side_effects=True, vmem_limit_bytes=48 << 20
        ),
        name="front",
    )(x, offsets, band_bins, dead)


def stack_group(gi, gj, out, lhs):
    at_rows = pl.ds(pl.multiple_of(pl.program_id(0) * 16, 16), 16)
    xj = gj[:, :, at_rows, :].reshape(16, 16, 256).astype(F32)
    flipped = jnp.concatenate([-xj[:, 8:], xj[:, :8]], axis=1)
    bin_of = lax.broadcasted_iota(jnp.int32, (256, 256), 1) & 3
    for s, rows in enumerate((xj, flipped)):
        turned_rows = rows.reshape(256, 256).T
        for b in range(4):
            at = (s * 4 + b) * 256
            lhs[at : at + 256] = jnp.where(bin_of == b, turned_rows, 0.0).astype(BF16)
    scale = 1.0 / math.sqrt(WIN)
    for h in range(2):
        right = gi[:, h, at_rows, :].reshape(256, 256)
        made = jnp.dot(lhs[...], right, preferred_element_type=F32) * scale
        out[:, :, :, h * 256 : (h + 1) * 256] = made.astype(BF16).reshape(2, 4, 256, 256)


def stack_call(gi, gj):
    vmem = pl.BlockSpec(memory_space=pltpu.VMEM)
    return pl.pallas_call(
        stack_group,
        out_shape=jax.ShapeDtypeStruct((2, NB, 256, 512), BF16),
        grid=(5,),
        in_specs=[vmem, vmem],
        out_specs=pl.BlockSpec((2, 4, 256, 512), lambda g: (0, g, 0, 0)),
        scratch_shapes=[pltpu.VMEM((2048, 256), BF16)],
        compiler_params=pltpu.CompilerParams(vmem_limit_bytes=32 << 20),
        name="stack",
    )(gi, gj)


def shards(recording, offsets, band_bins, dead_flags):
    placed = [
        pltpu.with_memory_space_constraint(a, pltpu.HBM)
        for a in (recording.T, offsets, band_bins, dead_flags.reshape(1, -1))
    ]
    gi, gj = front_call(*placed)
    return stack_call(gi, gj)


def solution(mesh):
    return jax.shard_map(
        shards,
        mesh=mesh,
        in_specs=(P("chan", "tm"), P(), P(), P("chan")),
        out_specs=P(None, None, "tm", "chan"),
        check_vma=False,
    )
```

```python
import functools
import math

import jax
import jax.numpy as jnp
from jax import lax
from jax.experimental import pallas as pl
from jax.experimental.pallas import tpu as pltpu
from jax.sharding import PartitionSpec as P

L = 15000
NB = 20
HOP = L // 2
TWO_PI = 2.0 * math.pi
FLOOR = 0.7
WIN = 32
STEP = 1024
CHUNKS = 15
ROWS = 40
AHEAD = 6
F32 = jnp.float32
BF16 = jnp.bfloat16


def bin_rows(bins):
    row = lax.broadcasted_iota(jnp.int32, (24, 128), 0)
    out = jnp.zeros((24, 128), jnp.int32)
    for b in range(NB):
        hit = row == b
        if b >= 16:
            hit = hit | (row == b + 4)
        out = jnp.where(hit, bins[b], out)
    return out.astype(F32)


def turned(turns):
    whole = jnp.floor(turns * (1.0 / L))
    rest = turns - whole * float(L)
    rest = jnp.where(rest < 0.0, rest + float(L), rest)
    rest = jnp.where(rest >= float(L), rest - float(L), rest)
    angle = rest * (TWO_PI / L)
    return jnp.cos(angle), jnp.sin(angle)


def start_state(bins, first):
    lane = lax.broadcasted_iota(jnp.int32, (24, 128), 1)
    row = lax.broadcasted_iota(jnp.int32, (24, 128), 0)
    place = (lane + (first + L)).astype(F32)
    quarter = jnp.where(row >= 20, float(L // 4), 0.0)
    cosine, sine = turned(bins * place + quarter)
    scale = 1.0 / math.sqrt(L)
    return cosine * scale, -sine * scale


def turn_on(state, step):
    v, q = state
    c, s = step
    return v * c + q * s, q * c - v * s


def table_rows(state, keep):
    v, q = state
    rows = jnp.concatenate([v[:16], q[:16], v[16:]], axis=0)
    return rows if keep is None else jnp.where(keep, rows, 0.0)


def regroup():
    d = lax.broadcasted_iota(jnp.int32, (80, 80), 0)
    s = lax.broadcasted_iota(jnp.int32, (80, 80), 1)
    p, w = (d >> 3) & 1, (d >> 2) & 1
    b = (d >> 4) * 4 + (d & 3)
    source = w * ROWS + jnp.where(b < 16, p * 16 + b, 32 + p * 4 + (b - 16))
    return jnp.where(s == source, 1.0, 0.0).astype(BF16)


def front(
    x_hbm, offs_hbm, bins_hbm, dead_hbm, gi, gj,
    xbuf, tab, offs, bins_ref, dead, own, sums, back, recv,
    x_sems, small_sems, send_sems, back_sems, i_sems, j_sems,
):
    c = lax.axis_index("chan")
    t = lax.axis_index("tm")
    z, xl = c // 2, c % 2
    y, xh, core = t // 4, (t // 2) % 2, t % 2
    sent = []

    def send(source, target, recv_sem, device):
        copy = pltpu.make_async_remote_copy(
            src_ref=source,
            dst_ref=target,
            send_sem=send_sems.at[len(sent)],
            recv_sem=recv_sem,
            device_id=device,
            device_id_type=pl.DeviceIdType.MESH,
        )
        copy.start()
        sent.append(copy)
        return copy

    def block_of(yy, hi, k):
        return 4 * (yy % 4) + 2 * hi + k

    up, down = (c, block_of(y + 1, xh, core)), (c, block_of(y + 3, xh, core))
    across, other = (c, block_of(y, 1 - xh, core)), (c, block_of(y, xh, 1 - core))
    z_up, z_down = ((c + 2) % 8, t), ((c + 6) % 8, t)
    previous, following = (c, (t + 15) % 16), (c, (t + 1) % 16)

    small = [
        pltpu.make_async_copy(src, dst, small_sems.at[n])
        for n, (src, dst) in enumerate(((offs_hbm, offs), (bins_hbm, bins_ref), (dead_hbm, dead)))
    ]
    for copy in small:
        copy.start()

    def chunk_copy(g):
        rows = STEP if isinstance(g, jax.Array) or g < CHUNKS - 1 else L - STEP * (CHUNKS - 1)
        at = pl.ds(pl.multiple_of(g * STEP, STEP), rows)
        return pltpu.make_async_copy(x_hbm.at[at], xbuf.at[at], x_sems.at[g])

    tail = (L // 16) * 16
    for g in range(AHEAD):
        chunk_copy(g).start()

    barrier = pltpu.get_barrier_semaphore()
    side = (2 * z + 1 - xl, t)
    sources = [up, down, across, other, z_up, z_down, side, following]
    sources += [(2 * y + xh, block_of(2 * y + 6 - z, xl, k)) for k in range(2)]
    for device in sources:
        pl.semaphore_signal(
            barrier, inc=1, device_id=device, device_id_type=pl.DeviceIdType.MESH
        )

    xbuf[pl.ds(tail, CHUNKS * STEP - tail)] = jnp.zeros((CHUNKS * STEP - tail, 512), BF16)
    own[...] = jnp.zeros_like(own)
    back[...] = jnp.zeros_like(back)
    sums[...] = jnp.zeros_like(sums)
    for copy in small:
        copy.wait()

    before = 2 * jnp.maximum(t - 1, 0)
    off0, off1 = offs[2 * t], offs[2 * t + 1]
    boff0, boff1 = offs[before], offs[before + 1]
    a0, a1 = off0, HOP + off1
    e0, e1 = boff0, HOP + boff1
    bins = bin_rows(bins_ref)
    step = turned(bins * 128.0)

    low = jnp.zeros((16, STEP), jnp.int32)
    high = jnp.zeros((16, STEP), jnp.int32)
    row = lax.broadcasted_iota(jnp.int32, (16, STEP), 0)
    for r, (lo, hi) in enumerate(((a0, L), (a1, L), (0, e0), (0, e1))):
        low = jnp.where(row == r, lo, low)
        high = jnp.where(row == r, hi, high)
    inner = lax.broadcasted_iota(jnp.int32, (16, STEP), 1)
    lane = lax.broadcasted_iota(jnp.int32, (ROWS, 128), 1)

    def chunk(g, slot, states, limits, targets, energies):
        states = list(states)
        tables = len(limits)
        height = 48 if tables == 1 else 80
        for k in range(STEP // 128):
            place = lane + (g * STEP + k * 128)
            rows = []
            for n, limit in enumerate(limits):
                keep = None
                if limit is not None:
                    keep = place >= limit[1] if limit[0] else place < limit[1]
                rows.append(table_rows(states[n], keep))
                states[n] = turn_on(states[n], step)
            if tables == 1:
                rows.append(jnp.zeros((8, 128), F32))
            tab[slot, 0:height, k * 128 : (k + 1) * 128] = jnp.concatenate(rows, axis=0).astype(BF16)
        x = xbuf[pl.ds(pl.multiple_of(g * STEP, STEP), STEP), :]
        raw = jnp.dot(tab[slot, 0:height, :], x, preferred_element_type=F32)
        for n, target in enumerate(targets):
            target[0:ROWS] += raw[n * ROWS : (n + 1) * ROWS]
        if energies:
            place = inner + g * STEP
            mask = jnp.where((place >= low) & (place < high), 1.0, 0.0).astype(BF16)
            sums[...] += jnp.dot(mask, x * x, preferred_element_type=F32)[0:8]
        return tuple(states)

    own0, own1 = own.at[0], own.at[1]
    back0, back1 = back.at[0], back.at[1]
    states = (start_state(bins, L - e0), start_state(bins, L - e1))
    for g in range(4):
        chunk_copy(g).wait()
        if g + AHEAD < CHUNKS:
            chunk_copy(g + AHEAD).start()
        states = chunk(g, g % 2, states, ((False, e0), None), (back0, back1), True)
    back[0, 40:41] = sums[2:3]
    pl.semaphore_wait(barrier, len(sources))
    early = send(back.at[0], recv.at[0], back_sems.at[0], previous)
    states = states[1:]
    s_own0 = start_state(bins, -a0)
    s_own1 = start_state(bins, 7 * STEP - a1)
    chunk_copy(4).wait()
    for g in range(4 + AHEAD, CHUNKS):
        chunk_copy(g).start()
    states = chunk(4, 0, states, ((False, e1),), (back1,), True)

    def pair(i, states):
        for k in range(2):
            chunk_copy(5 + 2 * i + k).wait()
        for k in range(2):
            states = chunk(5 + 2 * i + k, 1 - k, states, ((False, e1),), (back1,), True)
        return states

    lax.fori_loop(0, 3, pair, states)
    back[1, 40:41] = sums[3:4]
    late = send(back.at[1], recv.at[1], back_sems.at[1], previous)

    states = chunk(0, 0, (s_own0,), ((True, a0),), (own0,), False)

    def pair_own(i, states):
        for k in range(2):
            states = chunk(1 + 2 * i + k, 1 - k, states, ((True, a0),), (own0,), False)
        return states

    states = lax.fori_loop(0, 3, pair_own, states)
    for g in range(11, CHUNKS):
        chunk_copy(g).wait()
    both = (None, (True, a1))
    def pair_both(i, states):
        for k in range(2):
            states = chunk(7 + 2 * i + k, k, states, both, (own0, own1), False)
        return states

    def pair_last(i, states):
        for k in range(2):
            states = chunk(11 + 2 * i + k, k, states, both, (own0, own1), True)
        return states

    states = lax.fori_loop(0, 2, pair_both, states + (s_own1,))
    lax.fori_loop(0, 2, pair_last, states)

    matrix = regroup()
    alive = 1.0 - dead[...].astype(F32)
    early.wait_recv()
    late.wait_recv()
    white = []
    for w in range(2):
        more = jnp.where(t == 15, 0.0, recv[w])
        raw = own[w, 0:ROWS] + more[0:ROWS]
        energy = sums[w : w + 1] + more[40:41]
        spectra = raw / jnp.sqrt(energy / L + 1e-06)
        level = jnp.sum(spectra * spectra, axis=0, keepdims=True) * (1.0 / NB)
        white.append(spectra * (alive / jnp.sqrt(jnp.maximum(level, FLOOR))))
    white = jnp.concatenate(white, axis=0).astype(BF16)
    ordered = jnp.dot(matrix, white, preferred_element_type=F32).astype(BF16)
    for h in range(2):
        gi[t, h] = ordered[:, h * 256 : (h + 1) * 256]

    def give(block, h, device):
        send(gi.at[block, h], gi.at[block, h], i_sems.at[block, h], device)

    def got(block, h):
        pltpu.make_async_copy(gi.at[block, h], gi.at[block, h], i_sems.at[block, h]).wait()

    def pass_j(q, s, device):
        send(gj.at[q, s], gj.at[q, s], j_sems.at[q, s], device)

    def got_j(q, s):
        pltpu.make_async_copy(gj.at[q, s], gj.at[q, s], j_sems.at[q, s]).wait()

    halves = range(2)
    near = block_of(y, 1 - xh, core)
    below, above = block_of(y + 3, xh, core), block_of(y + 1, xh, core)
    far = block_of(y + 2, xh, core)
    near_below, near_above = block_of(y + 3, 1 - xh, core), block_of(y + 1, 1 - xh, core)
    near_far = block_of(y + 2, 1 - xh, core)
    q_of = [[2 * ((2 * y + k - z) % 4) + hi for hi in (xl, 1 - xl)] for k in (6, 7, 5, 8)]
    q_own, q_low, q_high, q_far = q_of

    for h in halves:
        send(
            gi.at[t, h],
            gj.at[t // 2, core],
            j_sems.at[t // 2, core],
            (2 * ((2 * z + 6 - y) % 4) + xh, block_of(z, xl, h)),
        )
    for h in halves:
        give(t, h, across)
    for h in halves:
        give(t, h, up)
        give(t, h, down)
    for h in halves:
        give(t, h, other)

    got(below, 0)
    give(below, 0, up)
    got(above, 1)
    give(above, 1, down)
    for h in halves:
        got(near, h)
        give(near, h, up)
        give(near, h, down)
    for s in halves:
        got_j(q_own[0], s)
        pass_j(q_own[0], s, side)
        pass_j(q_own[0], s, z_up)
        pass_j(q_own[0], s, z_down)
    got(below, 1)
    got(above, 0)
    for block in (below, above, near):
        for h in halves:
            give(block, h, other)
    got(near_below, 0)
    give(near_below, 0, up)
    got(near_above, 1)
    give(near_above, 1, down)
    got(near_below, 1)
    got(near_above, 0)
    for s in halves:
        got_j(q_own[1], s)
        pass_j(q_own[1], s, z_up)
        pass_j(q_own[1], s, z_down)
    got_j(q_low[0], 0)
    pass_j(q_low[0], 0, z_up)
    got_j(q_high[0], 1)
    pass_j(q_high[0], 1, z_down)
    for block in (near_below, near_above):
        for h in halves:
            give(block, h, other)
    for block in (far, near_far):
        for h in halves:
            got(block, h)
            give(block, h, other)
    got_j(q_low[1], 0)
    pass_j(q_low[1], 0, z_up)
    got_j(q_high[1], 1)
    pass_j(q_high[1], 1, z_down)
    for q_l, q_h in zip(q_low, q_high):
        got_j(q_l, 1)
        got_j(q_h, 0)
    for q in q_far:
        for s in halves:
            got_j(q, s)
    for yy in range(4):
        for hi in range(2):
            for h in halves:
                got(block_of(yy, hi, 1 - core), h)
    for copy in sent:
        copy.wait_send()


N_SENDS = 48


def front_call(x, offsets, band_bins, dead):
    anywhere = pl.BlockSpec(memory_space=pltpu.HBM)
    vmem = pl.BlockSpec(memory_space=pltpu.VMEM)
    return pl.pallas_call(
        front,
        out_shape=(
            jax.ShapeDtypeStruct((16, 2, 80, 256), BF16),
            jax.ShapeDtypeStruct((8, 2, 80, 256), BF16),
        ),
        in_specs=[anywhere] * 4,
        out_specs=(vmem, vmem),
        scratch_shapes=[
            pltpu.VMEM((CHUNKS * STEP, 512), BF16),
            pltpu.VMEM((2, 80, STEP), BF16),
            pltpu.SMEM((32,), jnp.int32),
            pltpu.SMEM((NB,), jnp.int32),
            pltpu.VMEM((1, 512), jnp.int32),
            pltpu.VMEM((2, ROWS, 512), F32),
            pltpu.VMEM((8, 512), F32),
            pltpu.VMEM((2, 48, 512), F32),
            pltpu.VMEM((2, 48, 512), F32),
            pltpu.SemaphoreType.DMA((CHUNKS,)),
            pltpu.SemaphoreType.DMA((3,)),
            pltpu.SemaphoreType.DMA((N_SENDS,)),
            pltpu.SemaphoreType.DMA((2,)),
            pltpu.SemaphoreType.DMA((16, 2)),
            pltpu.SemaphoreType.DMA((8, 2)),
        ],
        compiler_params=pltpu.CompilerParams(
            collective_id=0, has_side_effects=True, vmem_limit_bytes=48 << 20
        ),
        name="front",
    )(x, offsets, band_bins, dead)


def stack_all(gi, gj, out, lhs, made, sems):
    bin_of = lax.broadcasted_iota(jnp.int32, (256, 256), 1) & 3
    scale = 1.0 / math.sqrt(WIN)

    def left(g, s):
        rows = gj[:, :, g * 16 : g * 16 + 16, :].reshape(16, 16, 256).astype(F32)
        if s == 1:
            rows = jnp.concatenate([-rows[:, 8:], rows[:, :8]], axis=1)
        turned_rows = rows.reshape(256, 256).T
        for b in range(4):
            kept = jnp.where(bin_of == b, turned_rows, 0.0).astype(BF16)
            lhs[g % 2, s, b * 256 : b * 256 + 256] = kept

    copies = []
    left(0, 0)
    for g in range(5):
        for s in range(2):
            if s == 0:
                left(g, 1)
            elif g < 4:
                left(g + 1, 0)
            for h in range(2):
                right = gi[:, h, g * 16 : g * 16 + 16, :].reshape(256, 256)
                total = jnp.dot(lhs[g % 2, s], right, preferred_element_type=F32) * scale
                made[s, 4 * g : 4 * g + 4, :, h * 256 : (h + 1) * 256] = total.astype(BF16).reshape(
                    4, 256, 256
                )
            at = pl.ds(4 * g, 4)
            copy = pltpu.make_async_copy(made.at[s, at], out.at[s, at], sems.at[2 * g + s])
            copy.start()
            copies.append(copy)
    for copy in copies:
        copy.wait()


def stack_call(gi, gj):
    vmem = pl.BlockSpec(memory_space=pltpu.VMEM)
    return pl.pallas_call(
        stack_all,
        out_shape=jax.ShapeDtypeStruct((2, NB, 256, 512), BF16),
        in_specs=[vmem, vmem],
        out_specs=pl.BlockSpec(memory_space=pltpu.HBM),
        scratch_shapes=[
            pltpu.VMEM((2, 2, 1024, 256), BF16),
            pltpu.VMEM((2, NB, 256, 512), BF16),
            pltpu.SemaphoreType.DMA((10,)),
        ],
        compiler_params=pltpu.CompilerParams(vmem_limit_bytes=32 << 20),
        name="stack",
    )(gi, gj)


def shards(recording, offsets, band_bins, dead_flags):
    placed = [
        pltpu.with_memory_space_constraint(a, pltpu.HBM)
        for a in (recording.T, offsets, band_bins, dead_flags.reshape(1, -1))
    ]
    gi, gj = front_call(*placed)
    return stack_call(gi, gj)


def solution(mesh):
    return jax.shard_map(
        shards,
        mesh=mesh,
        in_specs=(P("chan", "tm"), P(), P(), P("chan")),
        out_specs=P(None, None, "tm", "chan"),
        check_vma=False,
    )
```

```python
import functools
import math

import jax
import jax.numpy as jnp
from jax import lax
from jax.experimental import pallas as pl
from jax.experimental.pallas import tpu as pltpu
from jax.sharding import PartitionSpec as P

L = 15000
NB = 20
HOP = L // 2
TWO_PI = 2.0 * math.pi
FLOOR = 0.7
WIN = 32
STEP = 1024
CHUNKS = 15
ROWS = 40
AHEAD = 6
F32 = jnp.float32
BF16 = jnp.bfloat16


def bin_rows(bins):
    row = lax.broadcasted_iota(jnp.int32, (24, 128), 0)
    out = jnp.zeros((24, 128), jnp.int32)
    for b in range(NB):
        hit = row == b
        if b >= 16:
            hit = hit | (row == b + 4)
        out = jnp.where(hit, bins[b], out)
    return out.astype(F32)


def turned(turns):
    whole = jnp.floor(turns * (1.0 / L))
    rest = turns - whole * float(L)
    rest = jnp.where(rest < 0.0, rest + float(L), rest)
    rest = jnp.where(rest >= float(L), rest - float(L), rest)
    angle = rest * (TWO_PI / L)
    return jnp.cos(angle), jnp.sin(angle)


def start_states(bins, firsts):
    lane = lax.broadcasted_iota(jnp.int32, (24, 128), 1)
    row = lax.broadcasted_iota(jnp.int32, (24, 128), 0)
    place = jnp.full((24, 128), 128, jnp.int32)
    for n, first in enumerate(firsts):
        place = jnp.where(lane == n, first + L, place)
    turn_c, turn_s = turned(bins * place.astype(F32))
    quarter = jnp.where(row >= 20, float(L // 4), 0.0)
    base_c, base_s = turned(bins * lane.astype(F32) + quarter)
    scale = 1.0 / math.sqrt(L)
    base_c, base_s = base_c * scale, base_s * scale
    states = []
    for n in range(len(firsts)):
        c = jnp.broadcast_to(turn_c[:, n : n + 1], (24, 128))
        s = jnp.broadcast_to(turn_s[:, n : n + 1], (24, 128))
        states.append((base_c * c - base_s * s, -(base_s * c + base_c * s)))
    at = len(firsts)
    step = (
        jnp.broadcast_to(turn_c[:, at : at + 1], (24, 128)),
        jnp.broadcast_to(turn_s[:, at : at + 1], (24, 128)),
    )
    return states, step


def turn_on(state, step):
    v, q = state
    c, s = step
    return v * c + q * s, q * c - v * s


def table_rows(state, keep):
    v, q = state
    rows = jnp.concatenate([v[:16], q[:16], v[16:]], axis=0)
    return rows if keep is None else jnp.where(keep, rows, 0.0)


def regroup():
    d = lax.broadcasted_iota(jnp.int32, (80, 80), 0)
    s = lax.broadcasted_iota(jnp.int32, (80, 80), 1)
    p, w = (d >> 3) & 1, (d >> 2) & 1
    b = (d >> 4) * 4 + (d & 3)
    source = w * ROWS + jnp.where(b < 16, p * 16 + b, 32 + p * 4 + (b - 16))
    return jnp.where(s == source, 1.0, 0.0).astype(BF16)


def front(
    x_hbm, offs_hbm, bins_hbm, dead_hbm, gi, gj,
    xbuf, tab, offs, bins_ref, dead, own, sums, back, recv,
    x_sems, small_sems, send_sems, back_sems, i_sems, j_sems,
):
    c = lax.axis_index("chan")
    t = lax.axis_index("tm")
    z, xl = c // 2, c % 2
    y, xh, core = t // 4, (t // 2) % 2, t % 2
    sent = []

    def send(source, target, recv_sem, device):
        copy = pltpu.make_async_remote_copy(
            src_ref=source,
            dst_ref=target,
            send_sem=send_sems.at[len(sent)],
            recv_sem=recv_sem,
            device_id=device,
            device_id_type=pl.DeviceIdType.MESH,
        )
        copy.start()
        sent.append(copy)
        return copy

    def block_of(yy, hi, k):
        return 4 * (yy % 4) + 2 * hi + k

    up, down = (c, block_of(y + 1, xh, core)), (c, block_of(y + 3, xh, core))
    across, other = (c, block_of(y, 1 - xh, core)), (c, block_of(y, xh, 1 - core))
    z_up, z_down = ((c + 2) % 8, t), ((c + 6) % 8, t)
    previous, following = (c, (t + 15) % 16), (c, (t + 1) % 16)

    small = [
        pltpu.make_async_copy(src, dst, small_sems.at[n])
        for n, (src, dst) in enumerate(((offs_hbm, offs), (bins_hbm, bins_ref), (dead_hbm, dead)))
    ]
    for copy in small:
        copy.start()

    def chunk_copy(g):
        rows = STEP if isinstance(g, jax.Array) or g < CHUNKS - 1 else L - STEP * (CHUNKS - 1)
        at = pl.ds(pl.multiple_of(g * STEP, STEP), rows)
        return pltpu.make_async_copy(x_hbm.at[at], xbuf.at[at], x_sems.at[g])

    tail = (L // 16) * 16
    for g in range(AHEAD):
        chunk_copy(g).start()

    barrier = pltpu.get_barrier_semaphore()
    side = (2 * z + 1 - xl, t)
    sources = [up, down, across, other, z_up, z_down, side, following]
    sources += [(2 * y + xh, block_of(2 * y + 6 - z, xl, k)) for k in range(2)]
    for device in sources:
        pl.semaphore_signal(
            barrier, inc=1, device_id=device, device_id_type=pl.DeviceIdType.MESH
        )

    xbuf[pl.ds(tail, CHUNKS * STEP - tail)] = jnp.zeros((CHUNKS * STEP - tail, 512), BF16)
    own[...] = jnp.zeros_like(own)
    back[...] = jnp.zeros_like(back)
    sums[...] = jnp.zeros_like(sums)
    for copy in small:
        copy.wait()

    before = 2 * jnp.maximum(t - 1, 0)
    off0, off1 = offs[2 * t], offs[2 * t + 1]
    boff0, boff1 = offs[before], offs[before + 1]
    a0, a1 = off0, HOP + off1
    e0, e1 = boff0, HOP + boff1
    bins = bin_rows(bins_ref)
    starts, step = start_states(bins, (L - e0, L - e1, -a0, 4 * STEP - a1))

    low = jnp.zeros((16, STEP), jnp.int32)
    high = jnp.zeros((16, STEP), jnp.int32)
    row = lax.broadcasted_iota(jnp.int32, (16, STEP), 0)
    for r, (lo, hi) in enumerate(((a0, L), (a1, L), (0, e0), (0, e1))):
        low = jnp.where(row == r, lo, low)
        high = jnp.where(row == r, hi, high)
    inner = lax.broadcasted_iota(jnp.int32, (16, STEP), 1)
    lane = lax.broadcasted_iota(jnp.int32, (ROWS, 128), 1)

    def chunk(g, slot, states, limits, targets, energies):
        states = list(states)
        tables = len(limits)
        height = 80 if tables == 2 else 128
        for k in range(STEP // 128):
            place = lane + (g * STEP + k * 128)
            rows = []
            for n, limit in enumerate(limits):
                keep = None
                if limit is not None:
                    keep = place >= limit[1] if limit[0] else place < limit[1]
                rows.append(table_rows(states[n], keep))
                states[n] = turn_on(states[n], step)
            if tables == 3:
                rows.append(jnp.zeros((8, 128), F32))
            tab[slot, 0:height, k * 128 : (k + 1) * 128] = jnp.concatenate(rows, axis=0).astype(BF16)
        x = xbuf[pl.ds(pl.multiple_of(g * STEP, STEP), STEP), :]
        raw = jnp.dot(tab[slot, 0:height, :], x, preferred_element_type=F32)
        for n, target in enumerate(targets):
            target[0:ROWS] += raw[n * ROWS : (n + 1) * ROWS]
        if energies:
            place = inner + g * STEP
            mask = jnp.where((place >= low) & (place < high), 1.0, 0.0).astype(BF16)
            sums[...] += jnp.dot(mask, x * x, preferred_element_type=F32)[0:8]
        return tuple(states)

    own0, own1 = own.at[0], own.at[1]
    back0, back1 = back.at[0], back.at[1]
    states = tuple(starts[:3])
    first_limits = ((False, e0), None, (True, a0))
    for g in range(4):
        chunk_copy(g).wait()
        if g + AHEAD < CHUNKS:
            chunk_copy(g + AHEAD).start()
        states = chunk(g, g % 2, states, first_limits, (back0, back1, own0), True)
    back[0, 40:41] = sums[2:3]
    pl.semaphore_wait(barrier, len(sources))
    early = send(back.at[0], recv.at[0], back_sems.at[0], previous)
    states = states[1:] + (starts[3],)
    limits = ((False, e1), None, (True, a1))
    targets = (back1, own0, own1)
    chunk_copy(4).wait()
    for g in range(4 + AHEAD, CHUNKS):
        chunk_copy(g).start()
    states = chunk(4, 0, states, limits, targets, True)

    def pair(i, states):
        for k in range(2):
            chunk_copy(5 + 2 * i + k).wait()
        for k in range(2):
            states = chunk(5 + 2 * i + k, 1 - k, states, limits, targets, True)
        return states

    states = lax.fori_loop(0, 3, pair, states)
    back[1, 40:41] = sums[3:4]
    late = send(back.at[1], recv.at[1], back_sems.at[1], previous)

    states = states[1:]
    for g in range(11, CHUNKS):
        chunk_copy(g).wait()

    def pair_last(i, states):
        for k in range(2):
            states = chunk(11 + 2 * i + k, k, states, (None, (True, a1)), (own0, own1), True)
        return states

    lax.fori_loop(0, 2, pair_last, states)

    matrix = regroup()
    alive = 1.0 - dead[...].astype(F32)
    early.wait_recv()
    late.wait_recv()
    white = []
    for w in range(2):
        more = jnp.where(t == 15, 0.0, recv[w])
        raw = own[w, 0:ROWS] + more[0:ROWS]
        energy = sums[w : w + 1] + more[40:41]
        spectra = raw / jnp.sqrt(energy / L + 1e-06)
        level = jnp.sum(spectra * spectra, axis=0, keepdims=True) * (1.0 / NB)
        white.append(spectra * (alive / jnp.sqrt(jnp.maximum(level, FLOOR))))
    white = jnp.concatenate(white, axis=0).astype(BF16)
    ordered = jnp.dot(matrix, white, preferred_element_type=F32).astype(BF16)
    for h in range(2):
        gi[t, h] = ordered[:, h * 256 : (h + 1) * 256]

    def give(block, h, device):
        send(gi.at[block, h], gi.at[block, h], i_sems.at[block, h], device)

    def got(block, h):
        pltpu.make_async_copy(gi.at[block, h], gi.at[block, h], i_sems.at[block, h]).wait()

    def pass_j(q, s, device):
        send(gj.at[q, s], gj.at[q, s], j_sems.at[q, s], device)

    def got_j(q, s):
        pltpu.make_async_copy(gj.at[q, s], gj.at[q, s], j_sems.at[q, s]).wait()

    halves = range(2)
    near = block_of(y, 1 - xh, core)
    below, above = block_of(y + 3, xh, core), block_of(y + 1, xh, core)
    far = block_of(y + 2, xh, core)
    near_below, near_above = block_of(y + 3, 1 - xh, core), block_of(y + 1, 1 - xh, core)
    near_far = block_of(y + 2, 1 - xh, core)
    q_of = [[2 * ((2 * y + k - z) % 4) + hi for hi in (xl, 1 - xl)] for k in (6, 7, 5, 8)]
    q_own, q_low, q_high, q_far = q_of

    for h in halves:
        send(
            gi.at[t, h],
            gj.at[t // 2, core],
            j_sems.at[t // 2, core],
            (2 * ((2 * z + 6 - y) % 4) + xh, block_of(z, xl, h)),
        )
    for h in halves:
        give(t, h, across)
    for h in halves:
        give(t, h, up)
        give(t, h, down)
    for h in halves:
        give(t, h, other)

    got(below, 0)
    give(below, 0, up)
    got(above, 1)
    give(above, 1, down)
    for h in halves:
        got(near, h)
        give(near, h, up)
        give(near, h, down)
    for s in halves:
        got_j(q_own[0], s)
        pass_j(q_own[0], s, side)
        pass_j(q_own[0], s, z_up)
        pass_j(q_own[0], s, z_down)
    got(below, 1)
    got(above, 0)
    for block in (below, above, near):
        for h in halves:
            give(block, h, other)
    got(near_below, 0)
    give(near_below, 0, up)
    got(near_above, 1)
    give(near_above, 1, down)
    got(near_below, 1)
    got(near_above, 0)
    for s in halves:
        got_j(q_own[1], s)
        pass_j(q_own[1], s, z_up)
        pass_j(q_own[1], s, z_down)
    got_j(q_low[0], 0)
    pass_j(q_low[0], 0, z_up)
    got_j(q_high[0], 1)
    pass_j(q_high[0], 1, z_down)
    for block in (near_below, near_above):
        for h in halves:
            give(block, h, other)
    for block in (far, near_far):
        for h in halves:
            got(block, h)
            give(block, h, other)
    got_j(q_low[1], 0)
    pass_j(q_low[1], 0, z_up)
    got_j(q_high[1], 1)
    pass_j(q_high[1], 1, z_down)
    for q_l, q_h in zip(q_low, q_high):
        got_j(q_l, 1)
        got_j(q_h, 0)
    for q in q_far:
        for s in halves:
            got_j(q, s)
    for yy in range(4):
        for hi in range(2):
            for h in halves:
                got(block_of(yy, hi, 1 - core), h)
    for copy in sent:
        copy.wait_send()


N_SENDS = 48


def front_call(x, offsets, band_bins, dead):
    anywhere = pl.BlockSpec(memory_space=pltpu.HBM)
    vmem = pl.BlockSpec(memory_space=pltpu.VMEM)
    return pl.pallas_call(
        front,
        out_shape=(
            jax.ShapeDtypeStruct((16, 2, 80, 256), BF16),
            jax.ShapeDtypeStruct((8, 2, 80, 256), BF16),
        ),
        in_specs=[anywhere] * 4,
        out_specs=(vmem, vmem),
        scratch_shapes=[
            pltpu.VMEM((CHUNKS * STEP, 512), BF16),
            pltpu.VMEM((2, 128, STEP), BF16),
            pltpu.SMEM((32,), jnp.int32),
            pltpu.SMEM((NB,), jnp.int32),
            pltpu.VMEM((1, 512), jnp.int32),
            pltpu.VMEM((2, ROWS, 512), F32),
            pltpu.VMEM((8, 512), F32),
            pltpu.VMEM((2, 48, 512), F32),
            pltpu.VMEM((2, 48, 512), F32),
            pltpu.SemaphoreType.DMA((CHUNKS,)),
            pltpu.SemaphoreType.DMA((3,)),
            pltpu.SemaphoreType.DMA((N_SENDS,)),
            pltpu.SemaphoreType.DMA((2,)),
            pltpu.SemaphoreType.DMA((16, 2)),
            pltpu.SemaphoreType.DMA((8, 2)),
        ],
        compiler_params=pltpu.CompilerParams(
            collective_id=0, has_side_effects=True, vmem_limit_bytes=48 << 20
        ),
        name="front",
    )(x, offsets, band_bins, dead)


def stack_all(gi, gj, out, lhs, made, sems):
    bin_of = lax.broadcasted_iota(jnp.int32, (256, 256), 1) & 3
    scale = 1.0 / math.sqrt(WIN)

    def left(g, s):
        rows = gj[:, :, g * 16 : g * 16 + 16, :].reshape(16, 16, 256).astype(F32)
        if s == 1:
            rows = jnp.concatenate([-rows[:, 8:], rows[:, :8]], axis=1)
        turned_rows = rows.reshape(256, 256).T
        for b in range(4):
            kept = jnp.where(bin_of == b, turned_rows, 0.0).astype(BF16)
            lhs[g % 2, s, b * 256 : b * 256 + 256] = kept

    copies = []
    left(0, 0)
    for g in range(5):
        for s in range(2):
            if s == 0:
                left(g, 1)
            elif g < 4:
                left(g + 1, 0)
            for h in range(2):
                right = gi[:, h, g * 16 : g * 16 + 16, :].reshape(256, 256)
                total = jnp.dot(lhs[g % 2, s], right, preferred_element_type=F32) * scale
                made[s, 4 * g : 4 * g + 4, :, h * 256 : (h + 1) * 256] = total.astype(BF16).reshape(
                    4, 256, 256
                )
            at = pl.ds(4 * g, 4)
            copy = pltpu.make_async_copy(made.at[s, at], out.at[s, at], sems.at[2 * g + s])
            copy.start()
            copies.append(copy)
    for copy in copies:
        copy.wait()


def stack_call(gi, gj):
    vmem = pl.BlockSpec(memory_space=pltpu.VMEM)
    return pl.pallas_call(
        stack_all,
        out_shape=jax.ShapeDtypeStruct((2, NB, 256, 512), BF16),
        in_specs=[vmem, vmem],
        out_specs=pl.BlockSpec(memory_space=pltpu.HBM),
        scratch_shapes=[
            pltpu.VMEM((2, 2, 1024, 256), BF16),
            pltpu.VMEM((2, NB, 256, 512), BF16),
            pltpu.SemaphoreType.DMA((10,)),
        ],
        compiler_params=pltpu.CompilerParams(vmem_limit_bytes=32 << 20),
        name="stack",
    )(gi, gj)


def shards(recording, offsets, band_bins, dead_flags):
    placed = [
        pltpu.with_memory_space_constraint(a, pltpu.HBM)
        for a in (recording.T, offsets, band_bins, dead_flags.reshape(1, -1))
    ]
    gi, gj = front_call(*placed)
    return stack_call(gi, gj)


def solution(mesh):
    return jax.shard_map(
        shards,
        mesh=mesh,
        in_specs=(P("chan", "tm"), P(), P(), P("chan")),
        out_specs=P(None, None, "tm", "chan"),
        check_vma=False,
    )
```

```python
import functools
import math

import jax
import jax.numpy as jnp
from jax import lax
from jax.experimental import pallas as pl
from jax.experimental.pallas import tpu as pltpu
from jax.sharding import PartitionSpec as P

L = 15000
NB = 20
HOP = L // 2
TWO_PI = 2.0 * math.pi
FLOOR = 0.7
WIN = 32
STEP = 1024
CHUNKS = 15
ROWS = 40
AHEAD = 6
F32 = jnp.float32
BF16 = jnp.bfloat16


def bin_rows(bins):
    row = lax.broadcasted_iota(jnp.int32, (24, 128), 0)
    out = jnp.zeros((24, 128), jnp.int32)
    for b in range(NB):
        hit = row == b
        if b >= 16:
            hit = hit | (row == b + 4)
        out = jnp.where(hit, bins[b], out)
    return out.astype(F32)


def turned(turns):
    whole = jnp.floor(turns * (1.0 / L))
    rest = turns - whole * float(L)
    rest = jnp.where(rest < 0.0, rest + float(L), rest)
    rest = jnp.where(rest >= float(L), rest - float(L), rest)
    angle = rest * (TWO_PI / L)
    return jnp.cos(angle), jnp.sin(angle)


def start_states(bins, firsts):
    lane = lax.broadcasted_iota(jnp.int32, (24, 128), 1)
    row = lax.broadcasted_iota(jnp.int32, (24, 128), 0)
    place = jnp.full((24, 128), 128, jnp.int32)
    for n, first in enumerate(firsts):
        place = jnp.where(lane == n, first + L, place)
    turn_c, turn_s = turned(bins * place.astype(F32))
    quarter = jnp.where(row >= 20, float(L // 4), 0.0)
    base_c, base_s = turned(bins * lane.astype(F32) + quarter)
    scale = 1.0 / math.sqrt(L)
    base_c, base_s = base_c * scale, base_s * scale
    states = []
    for n in range(len(firsts)):
        c = jnp.broadcast_to(turn_c[:, n : n + 1], (24, 128))
        s = jnp.broadcast_to(turn_s[:, n : n + 1], (24, 128))
        states.append((base_c * c - base_s * s, -(base_s * c + base_c * s)))
    at = len(firsts)
    step = (
        jnp.broadcast_to(turn_c[:, at : at + 1], (24, 128)),
        jnp.broadcast_to(turn_s[:, at : at + 1], (24, 128)),
    )
    return states, step


def turn_on(state, step):
    v, q = state
    c, s = step
    return v * c + q * s, q * c - v * s


def table_rows(state, keep):
    v, q = state
    rows = jnp.concatenate([v[:16], q[:16], v[16:]], axis=0)
    return rows if keep is None else jnp.where(keep, rows, 0.0)


def regroup():
    d = lax.broadcasted_iota(jnp.int32, (80, 80), 0)
    s = lax.broadcasted_iota(jnp.int32, (80, 80), 1)
    p, w = (d >> 3) & 1, (d >> 2) & 1
    b = (d >> 4) * 4 + (d & 3)
    source = w * ROWS + jnp.where(b < 16, p * 16 + b, 32 + p * 4 + (b - 16))
    return jnp.where(s == source, 1.0, 0.0).astype(BF16)


def front(
    x_hbm, offs_hbm, bins_hbm, dead_hbm, gi, gj,
    xbuf, tab, offs, bins_ref, dead, own, sums, back, recv, late_out, late_in,
    x_sems, small_sems, send_sems, back_sems, i_sems, j_sems,
):
    c = lax.axis_index("chan")
    t = lax.axis_index("tm")
    z, xl = c // 2, c % 2
    y, xh, core = t // 4, (t // 2) % 2, t % 2
    sent = []

    def send(source, target, recv_sem, device):
        copy = pltpu.make_async_remote_copy(
            src_ref=source,
            dst_ref=target,
            send_sem=send_sems.at[len(sent)],
            recv_sem=recv_sem,
            device_id=device,
            device_id_type=pl.DeviceIdType.MESH,
        )
        copy.start()
        sent.append(copy)
        return copy

    def block_of(yy, hi, k):
        return 4 * (yy % 4) + 2 * hi + k

    up, down = (c, block_of(y + 1, xh, core)), (c, block_of(y + 3, xh, core))
    across, other = (c, block_of(y, 1 - xh, core)), (c, block_of(y, xh, 1 - core))
    z_up, z_down = ((c + 2) % 8, t), ((c + 6) % 8, t)
    previous, following = (c, (t + 15) % 16), (c, (t + 1) % 16)

    small = [
        pltpu.make_async_copy(src, dst, small_sems.at[n])
        for n, (src, dst) in enumerate(((offs_hbm, offs), (bins_hbm, bins_ref), (dead_hbm, dead)))
    ]
    for copy in small:
        copy.start()

    def chunk_copy(g):
        rows = STEP if isinstance(g, jax.Array) or g < CHUNKS - 1 else L - STEP * (CHUNKS - 1)
        at = pl.ds(pl.multiple_of(g * STEP, STEP), rows)
        return pltpu.make_async_copy(x_hbm.at[at], xbuf.at[at], x_sems.at[g])

    tail = (L // 16) * 16
    for g in range(AHEAD):
        chunk_copy(g).start()

    barrier = pltpu.get_barrier_semaphore()
    side = (2 * z + 1 - xl, t)
    sources = [up, down, across, other, z_up, z_down, side, following]
    sources += [(2 * y + xh, block_of(2 * y + 6 - z, xl, k)) for k in range(2)]
    for device in sources:
        pl.semaphore_signal(
            barrier, inc=1, device_id=device, device_id_type=pl.DeviceIdType.MESH
        )

    xbuf[pl.ds(tail, CHUNKS * STEP - tail)] = jnp.zeros((CHUNKS * STEP - tail, 512), BF16)
    own[...] = jnp.zeros_like(own)
    back[...] = jnp.zeros_like(back)
    sums[...] = jnp.zeros_like(sums)
    for copy in small:
        copy.wait()

    before = 2 * jnp.maximum(t - 1, 0)
    off0, off1 = offs[2 * t], offs[2 * t + 1]
    boff0, boff1 = offs[before], offs[before + 1]
    a0, a1 = off0, HOP + off1
    e0, e1 = boff0, HOP + boff1
    bins = bin_rows(bins_ref)
    starts, step = start_states(bins, (L - e0, L - e1, -a0, 4 * STEP - a1))

    low = jnp.zeros((16, STEP), jnp.int32)
    high = jnp.zeros((16, STEP), jnp.int32)
    row = lax.broadcasted_iota(jnp.int32, (16, STEP), 0)
    for r, (lo, hi) in enumerate(((a0, L), (a1, L), (0, e0), (0, e1))):
        low = jnp.where(row == r, lo, low)
        high = jnp.where(row == r, hi, high)
    inner = lax.broadcasted_iota(jnp.int32, (16, STEP), 1)
    lane = lax.broadcasted_iota(jnp.int32, (ROWS, 128), 1)

    def chunk(g, slot, states, limits, targets, energies):
        states = list(states)
        tables = len(limits)
        height = 80 if tables == 2 else 128
        for k in range(STEP // 128):
            place = lane + (g * STEP + k * 128)
            rows = []
            for n, limit in enumerate(limits):
                keep = None
                if limit is not None:
                    keep = place >= limit[1] if limit[0] else place < limit[1]
                rows.append(table_rows(states[n], keep))
                states[n] = turn_on(states[n], step)
            if tables == 3:
                rows.append(jnp.zeros((8, 128), F32))
            tab[slot, 0:height, k * 128 : (k + 1) * 128] = jnp.concatenate(rows, axis=0).astype(BF16)
        x = xbuf[pl.ds(pl.multiple_of(g * STEP, STEP), STEP), :]
        raw = jnp.dot(tab[slot, 0:height, :], x, preferred_element_type=F32)
        for n, target in enumerate(targets):
            target[0:ROWS] += raw[n * ROWS : (n + 1) * ROWS]
        if energies:
            place = inner + g * STEP
            mask = jnp.where((place >= low) & (place < high), 1.0, 0.0).astype(BF16)
            sums[...] += jnp.dot(mask, x * x, preferred_element_type=F32)[0:8]
        return tuple(states)

    own0, own1 = own.at[0], own.at[1]
    back0, back1 = back.at[0], back.at[1]
    states = tuple(starts[:3])
    first_limits = ((False, e0), None, (True, a0))
    for g in range(4):
        chunk_copy(g).wait()
        if g + AHEAD < CHUNKS:
            chunk_copy(g + AHEAD).start()
        states = chunk(g, g % 2, states, first_limits, (back0, back1, own0), True)
    back[0, 40:41] = sums[2:3]
    pl.semaphore_wait(barrier, len(sources))
    early = send(back.at[0], recv.at[0], back_sems.at[0], previous)
    states = states[1:] + (starts[3],)
    limits = ((False, e1), None, (True, a1))
    targets = (back1, own0, own1)
    chunk_copy(4).wait()
    for g in range(4 + AHEAD, CHUNKS):
        chunk_copy(g).start()
    states = chunk(4, 0, states, limits, targets, True)

    def pair(i, states):
        for k in range(2):
            chunk_copy(5 + 2 * i + k).wait()
        for k in range(2):
            states = chunk(5 + 2 * i + k, 1 - k, states, limits, targets, True)
        return states

    states = lax.fori_loop(0, 3, pair, states)
    back[1, 40:41] = sums[3:4]
    late_out[...] = back[1, 0:ROWS].astype(BF16)
    tail_rows = pl.ds(ROWS, 8)
    late = send(late_out, late_in, back_sems.at[1], previous)
    late_energy = send(
        back.at[1, tail_rows], recv.at[1, tail_rows], back_sems.at[2], previous
    )

    states = states[1:]
    for g in range(11, CHUNKS):
        chunk_copy(g).wait()

    def pair_last(i, states):
        for k in range(2):
            states = chunk(11 + 2 * i + k, k, states, (None, (True, a1)), (own0, own1), True)
        return states

    lax.fori_loop(0, 2, pair_last, states)

    matrix = regroup()
    alive = 1.0 - dead[...].astype(F32)
    early.wait_recv()
    late.wait_recv()
    late_energy.wait_recv()
    white = []
    for w in range(2):
        more = late_in[...].astype(F32) if w == 1 else recv[0, 0:ROWS]
        raw = own[w, 0:ROWS] + jnp.where(t == 15, 0.0, more)
        energy = sums[w : w + 1] + jnp.where(t == 15, 0.0, recv[w, 40:41])
        spectra = raw / jnp.sqrt(energy / L + 1e-06)
        level = jnp.sum(spectra * spectra, axis=0, keepdims=True) * (1.0 / NB)
        white.append(spectra * (alive / jnp.sqrt(jnp.maximum(level, FLOOR))))
    white = jnp.concatenate(white, axis=0).astype(BF16)
    ordered = jnp.dot(matrix, white, preferred_element_type=F32).astype(BF16)
    for h in range(2):
        gi[t, h] = ordered[:, h * 256 : (h + 1) * 256]

    def give(block, h, device):
        send(gi.at[block, h], gi.at[block, h], i_sems.at[block, h], device)

    def got(block, h):
        pltpu.make_async_copy(gi.at[block, h], gi.at[block, h], i_sems.at[block, h]).wait()

    def pass_j(q, s, device):
        send(gj.at[q, s], gj.at[q, s], j_sems.at[q, s], device)

    def got_j(q, s):
        pltpu.make_async_copy(gj.at[q, s], gj.at[q, s], j_sems.at[q, s]).wait()

    halves = range(2)
    near = block_of(y, 1 - xh, core)
    below, above = block_of(y + 3, xh, core), block_of(y + 1, xh, core)
    far = block_of(y + 2, xh, core)
    near_below, near_above = block_of(y + 3, 1 - xh, core), block_of(y + 1, 1 - xh, core)
    near_far = block_of(y + 2, 1 - xh, core)
    q_of = [[2 * ((2 * y + k - z) % 4) + hi for hi in (xl, 1 - xl)] for k in (6, 7, 5, 8)]
    q_own, q_low, q_high, q_far = q_of

    for h in halves:
        send(
            gi.at[t, h],
            gj.at[t // 2, core],
            j_sems.at[t // 2, core],
            (2 * ((2 * z + 6 - y) % 4) + xh, block_of(z, xl, h)),
        )
    for h in halves:
        give(t, h, across)
    for h in halves:
        give(t, h, up)
        give(t, h, down)
    for h in halves:
        give(t, h, other)

    for h in halves:
        got(above, h)
        give(above, h, down)
    for h in halves:
        got(near, h)
        give(near, h, up)
        give(near, h, down)
    for s in halves:
        got_j(q_own[0], s)
        pass_j(q_own[0], s, side)
        pass_j(q_own[0], s, z_up)
        pass_j(q_own[0], s, z_down)
    for h in halves:
        got(below, h)
    for block in (below, above, near):
        for h in halves:
            give(block, h, other)
    for h in halves:
        got(near_above, h)
        give(near_above, h, down)
    for h in halves:
        got(near_below, h)
    for s in halves:
        got_j(q_own[1], s)
        pass_j(q_own[1], s, z_up)
        pass_j(q_own[1], s, z_down)
    got_j(q_low[0], 0)
    pass_j(q_low[0], 0, z_up)
    got_j(q_high[0], 1)
    pass_j(q_high[0], 1, z_down)
    for block in (near_below, near_above):
        for h in halves:
            give(block, h, other)
    for block in (far, near_far):
        for h in halves:
            got(block, h)
            give(block, h, other)
    got_j(q_low[1], 0)
    pass_j(q_low[1], 0, z_up)
    got_j(q_high[1], 1)
    pass_j(q_high[1], 1, z_down)
    for q_l, q_h in zip(q_low, q_high):
        got_j(q_l, 1)
        got_j(q_h, 0)
    for q in q_far:
        for s in halves:
            got_j(q, s)
    for yy in range(4):
        for hi in range(2):
            for h in halves:
                got(block_of(yy, hi, 1 - core), h)
    for copy in sent:
        copy.wait_send()


N_SENDS = 50


def front_call(x, offsets, band_bins, dead):
    anywhere = pl.BlockSpec(memory_space=pltpu.HBM)
    vmem = pl.BlockSpec(memory_space=pltpu.VMEM)
    return pl.pallas_call(
        front,
        out_shape=(
            jax.ShapeDtypeStruct((16, 2, 80, 256), BF16),
            jax.ShapeDtypeStruct((8, 2, 80, 256), BF16),
        ),
        in_specs=[anywhere] * 4,
        out_specs=(vmem, vmem),
        scratch_shapes=[
            pltpu.VMEM((CHUNKS * STEP, 512), BF16),
            pltpu.VMEM((2, 128, STEP), BF16),
            pltpu.SMEM((32,), jnp.int32),
            pltpu.SMEM((NB,), jnp.int32),
            pltpu.VMEM((1, 512), jnp.int32),
            pltpu.VMEM((2, ROWS, 512), F32),
            pltpu.VMEM((8, 512), F32),
            pltpu.VMEM((2, 48, 512), F32),
            pltpu.VMEM((2, 48, 512), F32),
            pltpu.VMEM((ROWS, 512), BF16),
            pltpu.VMEM((ROWS, 512), BF16),
            pltpu.SemaphoreType.DMA((CHUNKS,)),
            pltpu.SemaphoreType.DMA((3,)),
            pltpu.SemaphoreType.DMA((N_SENDS,)),
            pltpu.SemaphoreType.DMA((3,)),
            pltpu.SemaphoreType.DMA((16, 2)),
            pltpu.SemaphoreType.DMA((8, 2)),
        ],
        compiler_params=pltpu.CompilerParams(
            collective_id=0, has_side_effects=True, vmem_limit_bytes=48 << 20
        ),
        name="front",
    )(x, offsets, band_bins, dead)


def stack_all(gi, gj, out, lhs, made, sems):
    bin_of = lax.broadcasted_iota(jnp.int32, (256, 256), 1) & 3
    scale = 1.0 / math.sqrt(WIN)

    def left(g, s):
        rows = gj[:, :, g * 16 : g * 16 + 16, :].reshape(16, 16, 256).astype(F32)
        if s == 1:
            rows = jnp.concatenate([-rows[:, 8:], rows[:, :8]], axis=1)
        turned_rows = rows.reshape(256, 256).T
        for b in range(4):
            kept = jnp.where(bin_of == b, turned_rows, 0.0).astype(BF16)
            lhs[g % 2, s, b * 256 : b * 256 + 256] = kept

    copies = []
    left(0, 0)
    for g in range(5):
        for s in range(2):
            if s == 0:
                left(g, 1)
            elif g < 4:
                left(g + 1, 0)
            for h in range(2):
                right = gi[:, h, g * 16 : g * 16 + 16, :].reshape(256, 256)
                total = jnp.dot(lhs[g % 2, s], right, preferred_element_type=F32) * scale
                made[s, 4 * g : 4 * g + 4, :, h * 256 : (h + 1) * 256] = total.astype(BF16).reshape(
                    4, 256, 256
                )
            at = pl.ds(4 * g, 4)
            copy = pltpu.make_async_copy(made.at[s, at], out.at[s, at], sems.at[2 * g + s])
            copy.start()
            copies.append(copy)
    for copy in copies:
        copy.wait()


def stack_call(gi, gj):
    vmem = pl.BlockSpec(memory_space=pltpu.VMEM)
    return pl.pallas_call(
        stack_all,
        out_shape=jax.ShapeDtypeStruct((2, NB, 256, 512), BF16),
        in_specs=[vmem, vmem],
        out_specs=pl.BlockSpec(memory_space=pltpu.HBM),
        scratch_shapes=[
            pltpu.VMEM((2, 2, 1024, 256), BF16),
            pltpu.VMEM((2, NB, 256, 512), BF16),
            pltpu.SemaphoreType.DMA((10,)),
        ],
        compiler_params=pltpu.CompilerParams(vmem_limit_bytes=32 << 20),
        name="stack",
    )(gi, gj)


def shards(recording, offsets, band_bins, dead_flags):
    placed = [
        pltpu.with_memory_space_constraint(a, pltpu.HBM)
        for a in (recording.T, offsets, band_bins, dead_flags.reshape(1, -1))
    ]
    gi, gj = front_call(*placed)
    return stack_call(gi, gj)


def solution(mesh):
    return jax.shard_map(
        shards,
        mesh=mesh,
        in_specs=(P("chan", "tm"), P(), P(), P("chan")),
        out_specs=P(None, None, "tm", "chan"),
        check_vma=False,
    )
```
